32 devices in a mesh: gx: 4 (over y, core), gy: 4 (over z), gz: 2 (over x).
Axes of the slice: x: 2, y: 2, z: 4, core: 2. Of those that a mesh axis runs over, the one named last changes fastest.
Arguments:
- volume: bfloat16 [32, 32, 8, 32, 128], P('gx', 'gy', 'gz'), may hold values from -6 to 6
- conv_kernel: bfloat16 [3, 3, 3, 32, 64], replicated, may hold values from -0.21875 to 0.21875
- dense_one: bfloat16 [16, 16, 4, 64, 2048], P('gx', None, None, ('gy', 'gz')), may hold values from -0.0234375 to 0.0234375
- dense_two: float32 [2048, 256], replicated, may hold values from -0.125 to 0.125
- dense_three: float32 [256, 4], replicated, may hold values from -0.375 to 0.375
- targets: float32 [4, 128], replicated, may hold values from -3 to 3
Outputs:
- prediction: float32 [4, 128], replicated
- grad_dense_one: bfloat16 [16, 16, 4, 64, 2048], P('gx', None, None, ('gy', 'gz'))
- grad_conv: float32 [3, 3, 3, 32, 64], replicated
- grad_volume: bfloat16 [32, 32, 8, 32, 128], P('gx', 'gy', 'gz')
The draws below stay inside these ranges and needn't reach their ends.
All inputs are finite; a program needn't handle non-finite values.
Results may differ from the reference program's by a relative error of at most 0.008.
Values may be sent and summed in bfloat16 or wider, within the bound.
A program may use at most 128 MiB of HBM per device.

```python
import math
import jax
import jax.numpy as jnp
from jax import lax

BATCH = 128
CIN = 32
COUT = 64
HID1 = 2048
HID2 = 256
OUTS = 4
NX = 32
NY = 32
NZ = 8
MX = 16
MY = 16
MZ = 4


def steps_of(rng, shape, pieces, least, top_value):
    def one(position, shards_of):
        draws = jax.random.uniform(jax.random.fold_in(jax.random.fold_in(rng, 6), position), (shards_of,), jnp.float32, least / len(pieces), top_value / len(pieces))
        return jnp.repeat(jnp.exp(draws), shape[position] // shards_of).reshape((-1,) + (1,) * (len(shape) - position - 1))

    factor_of = one(*pieces[0])
    for cut in pieces[1:]:
        factor_of = factor_of * one(*cut)
    return factor_of


def gaussian(key, dims, scale, bound, pieces=(), held_as=jnp.bfloat16):
    values = jax.random.normal(key, dims, jnp.float32) * scale
    if len(pieces) > 0:
        values = steps_of(key, dims, pieces, -0.22, 0.18) * values
    return jnp.clip(values, min=-bound, max=bound).astype(held_as)


def setup_inputs(seed: int = 0) -> dict:
    seeds = jax.random.split(jax.random.key(seed), 7)
    volume = gaussian(seeds[0], (NX, NY, NZ, CIN, BATCH), 1.0, 6.0, ((0, 4), (1, 4), (2, 2)))
    conv_kernel = gaussian(seeds[1], (3, 3, 3, CIN, COUT), (27 * CIN) ** -0.5, 0.21875)
    dense_one = gaussian(seeds[2], (MX, MY, MZ, COUT, HID1), (MX * MY * MZ * COUT) ** -0.5, 0.0234375, ((0, 4), (3, 8)))
    dense_two = gaussian(seeds[3], (HID1, HID2), HID1 ** -0.5, 0.125, (), jnp.float32)
    dense_three = gaussian(seeds[4], (HID2, OUTS), HID2 ** -0.5, 0.375, (), jnp.float32)
    targets = gaussian(seeds[5], (OUTS, BATCH), 0.5, 3.0, (), jnp.float32)
    return {"volume": volume, "conv_kernel": conv_kernel, "dense_one": dense_one, "dense_two": dense_two, "dense_three": dense_three, "targets": targets}


loss_scale = 1024.0
leak_slope = 0.3

def smooth_leaky(values):
    return leak_slope * values + (1.0 - leak_slope) * jax.nn.softplus(values)

def leaky_derivative(values):
    return leak_slope + (1.0 - leak_slope) * jax.nn.sigmoid(values)

def conv_forward(padded, kernel):
    return lax.conv_general_dilated(padded, kernel, (1, 1, 1), 'VALID', dimension_numbers=('DHWCN', 'DHWIO', 'DHWCN'), preferred_element_type=jnp.float32)

def conv_back_input(padded_grad, kernel):
    flipped = kernel[::-1, ::-1, ::-1]
    return lax.conv_general_dilated(padded_grad, flipped, (1, 1, 1), 'VALID', dimension_numbers=('DHWCN', 'DHWOI', 'DHWCN'), preferred_element_type=jnp.float32)

def conv_back_kernel(padded, gradient):
    return lax.conv_general_dilated(padded, gradient, (1, 1, 1), 'VALID', dimension_numbers=('DHWNC', 'DHWOI', 'DHWNC'), preferred_element_type=jnp.float32)

def pooling(values):
    extent_x, extent_y, extent_z, channels, samples = values.shape
    return values.reshape(extent_x // 2, 2, extent_y // 2, 2, extent_z // 2, 2, channels, samples).mean(axis=(1, 3, 5))

def spread(values):
    extent_x, extent_y, extent_z, channels, samples = values.shape
    widened = jnp.broadcast_to(values[:, None, :, None, :, None], (extent_x, 2, extent_y, 2, extent_z, 2, channels, samples))
    return widened.reshape(2 * extent_x, 2 * extent_y, 2 * extent_z, channels, samples)

def split_samples(values, block_count, block_size):
    return jnp.moveaxis(values.reshape(values.shape[:4] + (block_count, block_size)), 4, 0)

def join_samples(values):
    moved = jnp.moveaxis(values, 0, 4)
    return moved.reshape(moved.shape[:4] + (moved.shape[4] * moved.shape[5],))

def reference(volume, conv_kernel, dense_one, dense_two, dense_three, targets):
    samples = volume.shape[4]
    block_size = math.gcd(samples, 16)
    block_count = samples // block_size
    rim = ((1, 1), (1, 1), (1, 1), (0, 0), (0, 0))
    blocks = split_samples(jnp.pad(volume, rim), block_count, block_size)

    def forward_block(padded):
        return pooling(smooth_leaky(conv_forward(padded, conv_kernel))).astype(jnp.bfloat16)
    pooled = join_samples(lax.map(forward_block, blocks))
    features = pooled.reshape(-1, samples)
    weights_flat = dense_one.reshape(-1, dense_one.shape[4])
    pre_one = lax.dot_general(weights_flat, features, (((0,), (0,)), ((), ())), preferred_element_type=jnp.float32)
    hidden_one = smooth_leaky(pre_one)
    pre_two = jnp.dot(dense_two.T, hidden_one, precision=lax.Precision.HIGHEST)
    hidden_two = smooth_leaky(pre_two)
    prediction = jnp.dot(dense_three.T, hidden_two, precision=lax.Precision.HIGHEST)
    error_grad = loss_scale * (prediction - targets)
    grad_pre_two = jnp.dot(dense_three, error_grad, precision=lax.Precision.HIGHEST) * leaky_derivative(pre_two)
    grad_pre_one = (jnp.dot(dense_two, grad_pre_two, precision=lax.Precision.HIGHEST) * leaky_derivative(pre_one)).astype(jnp.bfloat16)

    def slab_grad(slab):
        flat = slab.reshape(-1, samples)
        product = lax.dot_general(flat, grad_pre_one, (((1,), (1,)), ((), ())), preferred_element_type=jnp.float32)
        return (product / samples).astype(jnp.bfloat16).reshape(dense_one.shape[1:])
    grad_dense_one = lax.map(slab_grad, pooled)
    grad_features = jnp.dot(weights_flat, grad_pre_one, preferred_element_type=jnp.float32).astype(jnp.bfloat16)
    grad_blocks = split_samples(grad_features.reshape(pooled.shape), block_count, block_size)

    def backward_block(pair):
        padded, grad_pooled = pair
        conv_out = conv_forward(padded, conv_kernel)
        grad_out = (spread(grad_pooled.astype(jnp.float32)) / 8.0 * leaky_derivative(conv_out)).astype(jnp.bfloat16)
        grad_padded = jnp.pad(grad_out, rim)
        grad_input = conv_back_input(grad_padded, conv_kernel).astype(jnp.bfloat16)
        return (grad_input, conv_back_kernel(padded, grad_out))
    grad_inputs, grad_kernels = lax.map(backward_block, (blocks, grad_blocks))
    grad_conv = lax.optimization_barrier(jnp.sum(grad_kernels, axis=0)) / samples
    grad_volume = join_samples(grad_inputs)
    return (prediction, grad_dense_one, grad_conv, grad_volume)
```

```python
import jax
import jax.numpy as jnp
from jax import lax
from jax.sharding import PartitionSpec as P

loss_scale = 1024.0
leak_slope = 0.3
everyone = ("gx", "gy", "gz")


def summed(terms):
    devices = lax.axis_size(everyone)
    rows = terms.reshape(-1, terms.shape[-1])
    count = rows.shape[0]
    share = -(-count // (16 * devices)) * 16
    rows = jnp.pad(rows.astype(jnp.bfloat16), ((0, share * devices - count), (0, 0)))
    rows = rows.reshape(devices, share, -1)
    rows = lax.all_to_all(rows, everyone, split_axis=0, concat_axis=0, tiled=True)
    rows = jnp.sum(rows.astype(jnp.float32), axis=0)
    rows = lax.all_gather(rows, everyone, axis=0, tiled=True)
    return rows[:count].reshape(terms.shape)


def with_halo(array, sides, width):
    for axis, dim in sides:
        size, length = (lax.axis_size(axis), array.shape[dim])
        up = [(i, (i + 1) % size) for i in range(size - 1)]
        down = [(j, i) for i, j in up]
        last = lax.slice_in_dim(array, length - width, length, axis=dim)
        initial = lax.slice_in_dim(array, 0, width, axis=dim)
        before = lax.ppermute(last, axis, up)
        after = lax.ppermute(initial, axis, down)
        array = jnp.concatenate([before, array, after], axis=dim)
    return array


def smooth_leaky(values):
    return leak_slope * values + (1.0 - leak_slope) * jax.nn.softplus(values)


def leaky_derivative(values):
    return leak_slope + (1.0 - leak_slope) * jax.nn.sigmoid(values)


def conv_forward(padded, kernel):
    return lax.conv_general_dilated(
        padded,
        kernel,
        (1, 1, 1),
        "VALID",
        dimension_numbers=("DHWCN", "DHWIO", "DHWCN"),
        preferred_element_type=jnp.float32,
    )


def conv_back_input(padded_grad, kernel):
    flipped = kernel[::-1, ::-1, ::-1]
    return lax.conv_general_dilated(
        padded_grad,
        flipped,
        (1, 1, 1),
        "VALID",
        dimension_numbers=("DHWCN", "DHWOI", "DHWCN"),
        preferred_element_type=jnp.float32,
    )


def conv_back_kernel(padded, gradient):
    return lax.conv_general_dilated(
        padded,
        gradient,
        (1, 1, 1),
        "VALID",
        dimension_numbers=("DHWNC", "DHWOI", "DHWNC"),
        preferred_element_type=jnp.float32,
    )


def pooling(values):
    extent_x, extent_y, extent_z, channels, samples = values.shape
    return values.reshape(
        extent_x // 2, 2, extent_y // 2, 2, extent_z // 2, 2, channels, samples
    ).mean(axis=(1, 3, 5))


def spread(values):
    extent_x, extent_y, extent_z, channels, samples = values.shape
    widened = jnp.broadcast_to(
        values[:, None, :, None, :, None],
        (extent_x, 2, extent_y, 2, extent_z, 2, channels, samples),
    )
    return widened.reshape(2 * extent_x, 2 * extent_y, 2 * extent_z, channels, samples)


def body(volume, conv_kernel, dense_one, dense_two, dense_three, targets):
    padded = with_halo(volume, (("gx", 0), ("gy", 1), ("gz", 2)), 1)
    conv_out = conv_forward(padded, conv_kernel)
    pooled = pooling(smooth_leaky(conv_out)).astype(jnp.bfloat16)
    half_x, half_y, half_z, channels, samples = pooled.shape
    groups_y = lax.axis_size("gy")
    groups_z = lax.axis_size("gz")
    per_group = channels // (groups_y * groups_z)
    arrived = lax.all_to_all(pooled[None], ("gy", "gz"), split_axis=4, concat_axis=0, tiled=True)
    arrived = arrived.reshape(groups_y, groups_z, half_x, half_y, half_z, per_group, samples)
    weights_local = dense_one.reshape(
        half_x, groups_y, half_y, groups_z, half_z, per_group, dense_one.shape[4]
    )
    partial_one = jnp.einsum(
        "uvxyzcb,xuyvzch->bh", arrived, weights_local, preferred_element_type=jnp.float32
    )
    devices = lax.axis_size(everyone)
    share = samples // devices
    terms = partial_one.astype(jnp.bfloat16).reshape(devices, share, partial_one.shape[1])
    terms = lax.all_to_all(terms, everyone, split_axis=0, concat_axis=0, tiled=True)
    pre_one = jnp.sum(terms.astype(jnp.float32), axis=0)
    hidden_one = smooth_leaky(pre_one)
    pre_two = jnp.dot(hidden_one, dense_two, precision=lax.Precision.HIGHEST)
    hidden_two = smooth_leaky(pre_two)
    prediction = jnp.dot(hidden_two, dense_three, precision=lax.Precision.HIGHEST)
    own_targets = lax.dynamic_slice_in_dim(
        targets.T, lax.axis_index(everyone) * share, share, axis=0
    )
    error_grad = loss_scale * (prediction - own_targets)
    grad_pre_two = jnp.dot(
        error_grad, dense_three.T, precision=lax.Precision.HIGHEST
    ) * leaky_derivative(pre_two)
    grad_pre_one = (
        jnp.dot(grad_pre_two, dense_two.T, precision=lax.Precision.HIGHEST)
        * leaky_derivative(pre_one)
    ).astype(jnp.bfloat16)
    grad_pre_one = lax.all_gather(grad_pre_one, everyone, axis=0, tiled=False)
    grad_pre_one = grad_pre_one.reshape(samples, partial_one.shape[1])
    prediction = lax.all_gather(prediction, everyone, axis=0, tiled=True).T
    grad_local = jnp.einsum(
        "uvxyzcb,bh->xuyvzch", arrived, grad_pre_one, preferred_element_type=jnp.float32
    )
    grad_dense_one = (grad_local / samples).astype(jnp.bfloat16).reshape(dense_one.shape)
    grad_arrived = jnp.einsum(
        "xuyvzch,bh->uvxyzcb", weights_local, grad_pre_one, preferred_element_type=jnp.float32
    ).astype(jnp.bfloat16)
    outgoing = grad_arrived.reshape(groups_y * groups_z, half_x, half_y, half_z, per_group, samples)
    returned = lax.all_to_all(outgoing, ("gy", "gz"), split_axis=0, concat_axis=4, tiled=True)
    grad_pooled = returned.reshape(half_x, half_y, half_z, channels, samples)
    grad_out = (spread(grad_pooled.astype(jnp.float32)) / 8.0 * leaky_derivative(conv_out)).astype(
        jnp.bfloat16
    )
    grad_padded = with_halo(grad_out, (("gx", 0), ("gy", 1), ("gz", 2)), 1)
    grad_volume = conv_back_input(grad_padded, conv_kernel).astype(jnp.bfloat16)
    kernel_local = conv_back_kernel(padded, grad_out)
    grad_conv = summed(kernel_local) / samples
    return (prediction, grad_dense_one, grad_conv, grad_volume)


def solution(mesh):
    return jax.shard_map(
        body,
        mesh=mesh,
        in_specs=(
            P("gx", "gy", "gz", None, None),
            P(),
            P("gx", None, None, ("gy", "gz"), None),
            P(),
            P(),
            P(),
        ),
        out_specs=(
            P(),
            P("gx", None, None, ("gy", "gz"), None),
            P(),
            P("gx", "gy", "gz", None, None),
        ),
        check_vma=False,
    )
```
